32 devices in a mesh: dp: 4 (over z), fsdp: 8 (over y, x, core).
Axes of the slice: x: 2, y: 2, z: 4, core: 2. Of those that a mesh axis runs over, the one named last changes fastest.
Arguments:
- hidden_in: bfloat16 [32768, 768], P(('dp', 'fsdp')), may hold values from -6 to 6
- lengths: int32 [32], P(('dp', 'fsdp')), may hold values from 128 to 1024, as said below
- expert_ids: int32 [32768, 1], P(('dp', 'fsdp')), may hold values from 0 to 1; in each aligned block of 1024 rows (0 to 1023, 1024 to 2047, ...) at most 768 rows name the same one
- norm1_gain: bfloat16 [768], P(('dp', 'fsdp')), may hold values from 0.25 to 1.75
- norm1_bias: bfloat16 [768], P(('dp', 'fsdp')), may hold values from -2 to 2
- qkv_weight: bfloat16 [768, 2304], P(('dp', 'fsdp')), may hold values from -0.21875 to 0.21875
- attn_out_weight: bfloat16 [768, 768], P(('dp', 'fsdp')), may hold values from -1.75 to 1.75
- norm2_gain: bfloat16 [768], P(('dp', 'fsdp')), may hold values from 0.25 to 1.75
- norm2_bias: bfloat16 [768], P(('dp', 'fsdp')), may hold values from -2 to 2
- expert_in: bfloat16 [3072, 2, 768], P(('dp', 'fsdp')), may hold values from -0.21875 to 0.21875
- expert_out: bfloat16 [3072, 2, 768], P(('dp', 'fsdp')), may hold values from -0.109375 to 0.109375
- out_grad: bfloat16 [32768, 768], P(('dp', 'fsdp')), may hold values from -6 to 6
Outputs:
- hidden_out: bfloat16 [32768, 768], P(('dp', 'fsdp'))
- input_grad: bfloat16 [32768, 768], P(('dp', 'fsdp'))
- grad_norm1_gain: float32 [768], P(('dp', 'fsdp'))
- grad_norm1_bias: float32 [768], P(('dp', 'fsdp'))
- grad_qkv: float32 [768, 2304], P(('dp', 'fsdp'))
- grad_attn_out: float32 [768, 768], P(('dp', 'fsdp'))
- grad_norm2_gain: float32 [768], P(('dp', 'fsdp'))
- grad_norm2_bias: float32 [768], P(('dp', 'fsdp'))
- grad_expert_in: float32 [3072, 2, 768], P(('dp', 'fsdp'))
- grad_expert_out: float32 [3072, 2, 768], P(('dp', 'fsdp'))
The draws below stay inside these ranges and needn't reach their ends.
Inputs may be any that keep to these rules, and one draw needn't show every extreme that they name: `lengths`: rows of a sequence past its length are padding; in every draw one sequence has exactly 1024 valid tokens. `expert_ids`: among the rows of one device at most 768 name the same expert, and in every draw some device's expert receives exactly 768.
All inputs are finite; a program needn't handle non-finite values.
Results may differ from the reference program's by a relative error of at most 0.012.
Values may be sent and summed in bfloat16 or wider, within the bound.
A program may use at most 320 MiB of HBM per device.

```python
import math
import jax
import jax.numpy as jnp
import numpy as np
from jax import lax

D = 768
HEADS = 12
HEAD_DIM = 64
FF = 3072
EXPERTS = 2
SEQ_LEN = 1024
MIN_LEN = 128
CAP = 768
TOK_DEV = 1024
SEQS = 32
TOKENS = 32768


def draw_lengths(key, part):
    base_lengths = jax.random.randint(key, (SEQS,), MIN_LEN, SEQ_LEN + 1)
    longest = jax.random.randint(jax.random.fold_in(key, 11), (), 0, SEQS)
    return jnp.where(jnp.arange(SEQS) == longest, SEQ_LEN, base_lengths).astype(jnp.int32)


def spiked(entries, key, source, target, shards_of, factor):
    owner, partner = [(jnp.arange(entries.shape[axis_at]) // (entries.shape[axis_at] // shards_of)).reshape([-1 if axis == axis_at else 1 for axis in range(entries.ndim)]) for axis_at in (source, target)]
    chosen = jax.random.permutation(key, shards_of)[partner]
    strong = (owner == chosen) | (owner == (partner + shards_of // 2) % shards_of)
    return jnp.where(strong, factor * entries, entries)


def steps_of(key, dims, pieces, least, high):
    def one(axis_at, parts):
        steps = jax.random.uniform(jax.random.fold_in(jax.random.fold_in(key, 6), axis_at), (parts,), jnp.float32, least / len(pieces), high / len(pieces))
        return jnp.repeat(jnp.exp(steps), dims[axis_at] // parts).reshape((-1,) + (1,) * (len(dims) - axis_at - 1))

    factor_of = one(*pieces[0])
    for cut in pieces[1:]:
        factor_of = factor_of * one(*cut)
    return factor_of


def routed_block(key, own, number, rows, amount, top, reach, skew):
    sequence = jax.random.permutation(key, amount)
    packed, usual = portions_of(amount, rows * top, reach, skew, True), portions_of(amount, rows * top, reach, skew, False)
    places = jnp.arange(amount)

    def named(sizes, offset_by):
        used = int((sizes > 0).sum())
        fixed = max(1, used // 4)
        moved = fixed + (places - fixed + offset_by * (used - fixed)) % max(1, amount - fixed)
        return jnp.zeros((amount,), jnp.int32).at[sequence[jnp.where(places < fixed, places, moved)]].set(jnp.asarray(sizes, jnp.int32))

    sizes = jnp.where(number % 4 == 0, named(packed, number // 4), named(usual, number - number // 4 - 1))
    mixed = jax.random.permutation(jax.random.fold_in(own, 3), amount)
    donor, taker = mixed[0:amount // 2 * 2:2], mixed[1:amount // 2 * 2:2]
    margin = jnp.minimum(sizes[donor] - 1, reach - sizes[taker]) // 2
    margin = jnp.where((donor == sequence[0]) | (taker == sequence[0]) | (sizes[taker] == 0), 0, jnp.maximum(margin, 0))
    moved = jax.random.randint(jax.random.fold_in(own, 4), (amount // 2,), 0, 1 << 20) % (margin + 1)
    sizes = sizes.at[donor].add(-moved).at[taker].add(moved)
    labels = jnp.searchsorted(jnp.cumsum(sizes), jnp.arange(rows * top), side="right").astype(jnp.int32)
    listing = labels.reshape(top, rows).T
    listing = listing[jax.random.permutation(jax.random.fold_in(own, 1), rows)]
    offset_by = jax.random.randint(jax.random.fold_in(own, 2), (rows, 1), 0, top)
    return jnp.take_along_axis(listing, (jnp.arange(top)[None, :] + offset_by) % top, axis=1)


def portions_of(number_of, total, limit, lean, full):
    weights = [(1 << 20) // math.isqrt(standing ** lean) + 1 for standing in range(1, number_of + 1)]
    largest = limit if full else min(limit, max(-(-total // number_of), total * weights[0] // sum(weights)))
    least = 1 if total - largest >= number_of - 1 else 0
    holding, rest = [largest] + [least] * (number_of - 1), total - largest - least * (number_of - 1)
    while rest > 0:
        candidates = [i for i in range(1, number_of) if holding[i] < largest] or [i for i in range(1, number_of) if holding[i] < limit]
        pool, remaining = sum([weights[i] for i in candidates]), rest
        for i in candidates:
            more = min(limit - holding[i], max(1, remaining * weights[i] // pool), rest)
            holding[i] = holding[i] + more
            rest = rest - more
    return np.array(holding)


def scatter_about(stream_key, shape, spread, most, split=(), dtype=jnp.bfloat16):
    array = jax.random.normal(stream_key, shape, jnp.float32) * spread
    if len(split) > 0:
        array = steps_of(stream_key, shape, split, -0.22, 0.18) * array
    return jnp.clip(array, min=-most, max=most).astype(dtype)


def gaussian_with(stream_key, extent, spread, limit, cuts, heavy, kind=jnp.bfloat16):
    array = spread * jax.random.normal(stream_key, extent, jnp.float32)
    if cuts:
        array = array * steps_of(stream_key, extent, cuts, -0.22, 0.18)
    return jnp.clip(spiked(array, jax.random.fold_in(stream_key, 3), *heavy), -limit, limit).astype(kind)


def setup_inputs(seed: int = 0) -> dict:
    arg_keys = jax.random.split(jax.random.key(seed), 13)
    hidden_in = scatter_about(arg_keys[0], (TOKENS, D), 1.0, 6.0, ((0, 32),))
    lengths = draw_lengths(jax.random.fold_in(arg_keys[12], 71), 0)
    expert_ids_keys = jax.random.split(jax.random.fold_in(arg_keys[2], 1), TOKENS // TOK_DEV)
    expert_ids_turns = jax.random.permutation(jax.random.fold_in(arg_keys[2], 3), TOKENS // TOK_DEV)
    expert_ids = jax.vmap(lambda own, number: routed_block(jax.random.fold_in(arg_keys[2], 2), own, number, TOK_DEV, EXPERTS, 1, CAP, 1))(expert_ids_keys, expert_ids_turns).reshape((TOKENS, 1))
    norm1_gain = jnp.clip(1.0 + 0.15 * jax.random.normal(arg_keys[3], (D,), jnp.float32), 0.25, 1.75).astype(jnp.bfloat16)
    norm1_bias = scatter_about(arg_keys[4], (D,), 0.3, 2.0, ((0, 32),))
    qkv_weight = scatter_about(arg_keys[5], (D, 3 * D), D ** -0.5, 0.21875, ((0, 32),))
    attn_out_weight = scatter_about(arg_keys[6], (D, D), (max(D // 64, 1)) ** -0.5, 1.75, ((0, 32),))
    norm2_gain = jnp.clip(1.0 + 0.15 * jax.random.normal(arg_keys[7], (D,), jnp.float32), 0.25, 1.75).astype(jnp.bfloat16)
    norm2_bias = scatter_about(arg_keys[8], (D,), 0.3, 2.0, ((0, 32),))
    expert_in = scatter_about(arg_keys[9], (FF, EXPERTS, D), D ** -0.5, 0.21875, ((0, 32),))
    expert_out = scatter_about(arg_keys[10], (FF, EXPERTS, D), FF ** -0.5, 0.109375, ((0, 32),))
    out_grad = gaussian_with(arg_keys[11], (TOKENS, D), 1.0, 6.0, ((0, 32),), (0, 1, 32, 2.75))
    return {"hidden_in": hidden_in, "lengths": lengths, "expert_ids": expert_ids, "norm1_gain": norm1_gain, "norm1_bias": norm1_bias, "qkv_weight": qkv_weight, "attn_out_weight": attn_out_weight, "norm2_gain": norm2_gain, "norm2_bias": norm2_bias, "expert_in": expert_in, "expert_out": expert_out, "out_grad": out_grad}


@jax.custom_vjp
def low(v):
    return lax.optimization_barrier(v.astype(jnp.bfloat16)).astype(jnp.float32)

@jax.custom_vjp
def low_back(v):
    return v

def low_keep(v):
    return (low(v), None)

def low_pass(kept, grad):
    return (grad,)

def back_keep(v):
    return (v, None)

def back_low(kept, grad):
    return (low(grad),)
low.defvjp(low_keep, low_pass)
low_back.defvjp(back_keep, back_low)
epsilon = 1e-05
masked_score = -1e+30
gelu_coeff = 0.7978845608028654

def gelu_tanh(values):
    return 0.5 * values * (1.0 + jnp.tanh(gelu_coeff * (values + 0.044715 * values * values * values)))

def layer_norm(inputs, gain_vec, bias_vec):
    average = lax.optimization_barrier(jnp.mean(inputs, axis=-1, keepdims=True))
    centered = inputs - average
    variance = lax.optimization_barrier(jnp.mean(centered * centered, axis=-1, keepdims=True))
    return centered * lax.rsqrt(variance + epsilon) * gain_vec + bias_vec

def matmul(left, right):
    return jnp.dot(left, right, precision=lax.Precision.HIGHEST, preferred_element_type=jnp.float32)

def forward(inputs, params, seq_lengths, chosen):
    gain_one, bias_one, w_qkv, w_proj, gain_two, bias_two, w_in, w_out = params
    seq_count, length, model_width = inputs.shape
    flattened = inputs.reshape(seq_count * length, model_width)
    normed = low(layer_norm(flattened, gain_one, bias_one))
    joint = low(low_back(matmul(normed, w_qkv))).reshape(seq_count, length, 3, HEADS, HEAD_DIM)
    queries = joint[:, :, 0]
    keys_all = joint[:, :, 1]
    values_all = joint[:, :, 2]
    scores = jnp.einsum('sqhd,skhd->shqk', queries, keys_all, precision=lax.Precision.HIGHEST) * HEAD_DIM ** (-0.5)
    scores = low_back(scores)
    positions = jnp.arange(length)
    causal = (positions[None, :] <= positions[:, None])[None, None]
    inside = positions[None, None, None, :] < seq_lengths[:, None, None, None]
    scores = jnp.where(causal & inside, scores, masked_score)
    row_max = lax.optimization_barrier(jnp.max(scores, axis=-1, keepdims=True))
    exponent = jnp.exp(scores - row_max)
    probs = low(exponent / lax.optimization_barrier(jnp.sum(exponent, axis=-1, keepdims=True)))
    mixed_heads = jnp.einsum('shqk,skhd->sqhd', probs, values_all, precision=lax.Precision.HIGHEST)
    mixed_heads = low(low_back(mixed_heads.reshape(seq_count * length, model_width)))
    residual = flattened + low_back(matmul(mixed_heads, w_proj))
    normed_two = low(layer_norm(residual, gain_two, bias_two))
    picks = chosen.reshape(-1)
    branch = jnp.zeros_like(residual)
    for number in range(EXPERTS):
        preact = low_back(matmul(normed_two, w_in[:, number, :].T))
        activated = low(gelu_tanh(preact))
        branch = branch + jnp.where((picks == number)[:, None], matmul(activated, w_out[:, number, :]), 0.0)
    result = residual + low_back(branch)
    return result.reshape(seq_count, length, model_width)

def reference(hidden_in, lengths, expert_ids, norm1_gain, norm1_bias, qkv_weight, attn_out_weight, norm2_gain, norm2_bias, expert_in, expert_out, out_grad):
    group = math.gcd(SEQS, max(1, 2048 // SEQ_LEN))
    steps_count = SEQS // group
    params = (norm1_gain.astype(jnp.float32), norm1_bias.astype(jnp.float32), qkv_weight.astype(jnp.float32), attn_out_weight.astype(jnp.float32), norm2_gain.astype(jnp.float32), norm2_bias.astype(jnp.float32), expert_in.astype(jnp.float32), expert_out.astype(jnp.float32))
    inputs = hidden_in.astype(jnp.float32).reshape(steps_count, group, SEQ_LEN, D)
    cotangent = out_grad.astype(jnp.float32).reshape(steps_count, group, SEQ_LEN, D)
    seq_lengths = lengths.reshape(steps_count, group)
    picks = expert_ids.reshape(steps_count, group, SEQ_LEN)

    def group_step(totals, item):
        x_group, cot_group, len_group, pick_group = item
        result, pull = jax.vjp(lambda xval, pval: forward(xval, pval, len_group, pick_group), x_group, params)
        dinput, dparams = pull(cot_group)
        return (jax.tree.map(lambda left, right: left + right, totals, dparams), (result, dinput))
    zeroed = jax.tree.map(jnp.zeros_like, params)
    totals, (results, dinputs) = lax.scan(group_step, zeroed, (inputs, cotangent, seq_lengths, picks))
    return (results.reshape(TOKENS, D).astype(jnp.bfloat16), dinputs.reshape(TOKENS, D).astype(jnp.bfloat16), totals[0], totals[1], totals[2], totals[3], totals[4], totals[5], totals[6], totals[7])
```

```python
import functools

import jax
import jax.numpy as jnp
from jax import lax
from jax.experimental import pallas as pl
from jax.experimental.pallas import tpu as pltpu
from jax.sharding import PartitionSpec as P

HEAD_DIM = 64
CAP = 768
TILE = 256
PAIR = 128
epsilon = 1e-05
masked_score = -1e30
gelu_coeff = 0.7978845608028654
MESH = pl.DeviceIdType.MESH
F32 = jnp.float32
BF16 = jnp.bfloat16
NT = (((1,), (1,)), ((), ()))
TN = (((0,), (0,)), ((), ()))
VMEM_BYTES = 60 * 1024 * 1024


def dot(left, right):
    return jnp.dot(left, right, preferred_element_type=F32)


def dot_nt(left, right):
    return lax.dot_general(left, right, NT, preferred_element_type=F32)


def dot_tn(left, right):
    return lax.dot_general(left, right, TN, preferred_element_type=F32)


def norm_parts(values):
    average = jnp.mean(values, axis=-1, keepdims=True)
    centered = values - average
    variance = jnp.mean(centered * centered, axis=-1, keepdims=True)
    inverse = lax.rsqrt(variance + epsilon)
    return centered * inverse, inverse


def norm_back(grad, normal, inverse, gain):
    weighted = grad * gain
    first = jnp.mean(weighted, axis=-1, keepdims=True)
    second = jnp.mean(weighted * normal, axis=-1, keepdims=True)
    return inverse * (weighted - first - normal * second)


class Cube:
    def __init__(self, dp_size, fsdp_size):
        self.dp_size, self.fsdp_size = dp_size, fsdp_size
        self.count = dp_size * fsdp_size
        self.dp_bits = [("dp", b) for b in reversed(range(dp_size.bit_length() - 1))]
        self.fsdp_bits = [("fsdp", b) for b in reversed(range(1, fsdp_size.bit_length() - 1))]
        self.core = [("fsdp", 0)]
        self.orders = (
            self.dp_bits + self.fsdp_bits + self.core,
            self.dp_bits + self.fsdp_bits[::-1] + self.core,
            self.fsdp_bits + self.dp_bits + self.core,
        )

    def here(self):
        return lax.axis_index("dp"), lax.axis_index("fsdp")

    def partner(self, where, bit):
        axis, b = bit
        dp, fsdp = where
        if axis == "dp":
            return dp + self.step(dp, b), fsdp
        return dp, fsdp + self.step(fsdp, b)

    def step(self, value, b):
        return (1 << b) * (1 - 2 * lax.rem(lax.div(value, 1 << b), 2))

    def index(self, where, order, rel):
        dp, fsdp = where
        total = dp * self.fsdp_size + fsdp
        for k, (axis, b) in enumerate(order):
            if rel >> k & 1:
                total += self.step(dp, b) * self.fsdp_size if axis == "dp" else self.step(fsdp, b)
        return total

    def greet(self, where):
        barrier = pltpu.get_barrier_semaphore()
        bits = self.dp_bits + self.fsdp_bits + self.core
        for bit in bits:
            pl.semaphore_signal(
                barrier, inc=1, device_id=self.partner(where, bit), device_id_type=MESH
            )
        pl.semaphore_wait(barrier, len(bits))


class Gather:
    def __init__(self, cube, where, order, source, place, send_sems, recv_sems, own_sem):
        self.cube, self.where, self.order = cube, where, order
        self.source, self.place = source, place
        self.send_sems, self.recv_sems, self.own_sem = send_sems, recv_sems, own_sem
        self.levels = len(order)

    def copy(self, rel, k):
        target = rel | 1 << k
        index = self.cube.index(self.where, self.order, rel)
        return pltpu.make_async_remote_copy(
            src_ref=self.source if rel == 0 else self.place(index),
            dst_ref=self.place(index),
            send_sem=self.send_sems.at[target],
            recv_sem=self.recv_sems.at[target],
            device_id=self.cube.partner(self.where, self.order[k]),
            device_id_type=MESH,
        )

    def own(self):
        return pltpu.make_async_copy(
            self.source, self.place(self.cube.index(self.where, self.order, 0)), self.own_sem
        )

    def send_on(self, rel):
        for k in range(rel.bit_length(), self.levels):
            self.copy(rel, k).start()

    def arrive(self, rel):
        k = rel.bit_length() - 1
        self.copy(rel ^ 1 << k, k).wait_recv()

    def sent(self, rel):
        k = rel.bit_length() - 1
        self.copy(rel ^ 1 << k, k).wait_send()


def gather_kernel(cube, cuts, small, large, small_all, large_all, *sems):
    where = cube.here()
    cube.greet(where)
    flows = []
    spots = [("s", lo, hi, order) for lo, hi, order in cuts] + [("l", 0, 0, 0), ("l", 1, 1, 1)]
    for number, (kind, lo, hi, order) in enumerate(spots):
        send, recv, own = sems[3 * number : 3 * number + 3]
        if kind == "s":
            source = small.at[:, lo:hi]
            place = lambda index, lo=lo, hi=hi: small_all.at[index, :, lo:hi]
        else:
            source = large.at[lo]
            place = lambda index, lo=lo: large_all.at[index, lo]
        flows.append(Gather(cube, where, cube.orders[order], source, place, send, recv, own))
    groups = (flows[: len(cuts)], flows[len(cuts) :])
    for group in groups:
        for flow in group:
            flow.send_on(0)
            flow.own().start()
    for group in groups:
        for rel in range(1, cube.count):
            for flow in group:
                flow.arrive(rel)
                flow.send_on(rel)
    for flow in flows:
        flow.own().wait()
        for rel in range(1, cube.count):
            flow.sent(rel)


def gather_all(cube, small, large):
    count = cube.count
    columns = small.shape[1]
    lanes = columns // 128
    first, second = 128 * (lanes * 2 // 5), 128 * (lanes * 4 // 5)
    cuts = ((0, first, 0), (first, second, 1), (second, columns, 2))
    sems = []
    for _ in range(len(cuts) + 2):
        sems += [
            pltpu.SemaphoreType.DMA((count,)),
            pltpu.SemaphoreType.DMA((count,)),
            pltpu.SemaphoreType.DMA,
        ]
    return pl.pallas_call(
        functools.partial(gather_kernel, cube, cuts),
        out_shape=(
            jax.ShapeDtypeStruct((count,) + small.shape, small.dtype),
            jax.ShapeDtypeStruct((count,) + large.shape, large.dtype),
        ),
        in_specs=[pl.BlockSpec(memory_space=pl.ANY)] * 2,
        out_specs=(pl.BlockSpec(memory_space=pl.ANY),) * 2,
        scratch_shapes=sems,
        compiler_params=pltpu.CompilerParams(collective_id=0, has_side_effects=True),
    )(small, large)


class Reduce:
    def __init__(self, cube, where, order, part, kept, slot, send_sems, recv_sems, own_sems):
        self.cube, self.where, self.order = cube, where, order
        self.part, self.kept, self.slot = part, kept, slot
        self.send_sems, self.recv_sems, self.own_sems = send_sems, recv_sems, own_sems
        self.levels = len(order)
        self.half = cube.count // 2

    def copy(self, rel):
        k = rel.bit_length() - 1
        if rel >= self.half:
            source = self.part(self.cube.index(self.where, self.order, rel))
        else:
            source = self.kept(rel)
        return pltpu.make_async_remote_copy(
            src_ref=source,
            dst_ref=self.slot(rel),
            send_sem=self.send_sems.at[rel],
            recv_sem=self.recv_sems.at[rel],
            device_id=self.cube.partner(self.where, self.order[k]),
            device_id_type=MESH,
        )

    def own(self, rel):
        return pltpu.make_async_copy(
            self.part(self.cube.index(self.where, self.order, rel)),
            self.kept(rel),
            self.own_sems.at[rel],
        )

    def slots(self, rel):
        return [rel | 1 << k for k in range(rel.bit_length(), self.levels)]


def reduce_kernel(cube, cuts, parts, total, kept, slots, *sems):
    where = cube.here()
    cube.greet(where)
    flows = []
    for number, (lo, hi, order) in enumerate(cuts):
        send, recv, own = sems[3 * number : 3 * number + 3]
        flows.append(
            (
                lo,
                hi,
                Reduce(
                    cube,
                    where,
                    cube.orders[order],
                    lambda index, lo=lo, hi=hi: parts.at[index, :, :, lo:hi],
                    lambda rel, lo=lo, hi=hi: kept.at[rel, :, :, lo:hi],
                    lambda rel, lo=lo, hi=hi: slots.at[rel, :, :, lo:hi],
                    send,
                    recv,
                    own,
                ),
            )
        )
    half = cube.count // 2
    for rel in reversed(range(cube.count)):
        for _, _, flow in flows:
            if rel >= half:
                flow.copy(rel).start()
            else:
                flow.own(rel).start()
    units = kept.shape[1]
    for rel in reversed(range(half)):
        for lo, hi, flow in flows:
            flow.own(rel).wait()
            sources = flow.slots(rel)
            for other in sources:
                flow.copy(other).wait_recv()

            def add(unit, carry):
                value = kept[rel, unit, :, lo:hi].astype(F32)
                for other in sources:
                    value += slots[other, unit, :, lo:hi].astype(F32)
                if rel:
                    kept[rel, unit, :, lo:hi] = value.astype(BF16)
                else:
                    total[unit, :, lo:hi] = value
                return carry

            lax.fori_loop(0, units, add, 0)
            if rel:
                flow.copy(rel).start()
    for _, _, flow in flows:
        for rel in range(1, cube.count):
            flow.copy(rel).wait_send()


def reduce_all(cube, parts, cuts, collective_id):
    count = cube.count
    block = parts.shape[1:]
    sems = []
    for _ in cuts:
        sems += [pltpu.SemaphoreType.DMA((count,))] * 2
        sems += [pltpu.SemaphoreType.DMA((count // 2,))]
    return pl.pallas_call(
        functools.partial(reduce_kernel, cube, cuts),
        out_shape=jax.ShapeDtypeStruct(block, F32),
        in_specs=[pl.BlockSpec(memory_space=pl.ANY)],
        out_specs=pl.BlockSpec(memory_space=pltpu.VMEM),
        scratch_shapes=[
            pltpu.VMEM((count // 2,) + block, BF16),
            pltpu.VMEM((count,) + block, BF16),
        ]
        + sems,
        compiler_params=pltpu.CompilerParams(
            collective_id=collective_id, has_side_effects=True, vmem_limit_bytes=VMEM_BYTES
        ),
    )(parts)


def params(*semantics):
    return pltpu.CompilerParams(
        dimension_semantics=semantics or None, vmem_limit_bytes=VMEM_BYTES
    )


def norm_rows(ref):
    return jnp.transpose(ref[...].astype(F32))


def project_kernel(x_ref, w_ref, n_ref, normed_ref, joint_ref, rows):
    @pl.when(pl.program_id(0) == 0)
    def _():
        rows[...] = norm_rows(n_ref)

    normal, _ = norm_parts(x_ref[...].astype(F32))
    normed = (normal * rows[0:1] + rows[1:2]).astype(BF16)
    normed_ref[...] = normed
    joint_ref[...] = dot(normed, w_ref[...]).astype(BF16)


def project(inputs, whole):
    tokens, width = inputs.shape
    return pl.pallas_call(
        project_kernel,
        grid=(tokens // TILE,),
        out_shape=(
            jax.ShapeDtypeStruct((tokens, width), BF16),
            jax.ShapeDtypeStruct((tokens, 3 * width), BF16),
        ),
        in_specs=[
            pl.BlockSpec((TILE, width), lambda i: (i, 0)),
            pl.BlockSpec((width, 3 * width), lambda i: (0, 0)),
            pl.BlockSpec((width, 128), lambda i: (0, 4 * width // 128)),
        ],
        out_specs=(
            pl.BlockSpec((TILE, width), lambda i: (i, 0)),
            pl.BlockSpec((TILE, 3 * width), lambda i: (i, 0)),
        ),
        scratch_shapes=[pltpu.VMEM((128, width), F32)],
        compiler_params=params("arbitrary"),
    )(inputs, whole, whole)


def lane_iota(shape):
    return lax.broadcasted_iota(jnp.int32, shape, 1)


def row_iota(shape):
    return lax.broadcasted_iota(jnp.int32, shape, 0)


def attend_kernel(len_ref, q_ref, k_ref, v_ref, mixed_ref, lse_ref, keys):
    pair = pl.program_id(0)
    length = q_ref.shape[0]
    valid = len_ref[0]
    lane = lane_iota((length, PAIR))
    bias = jnp.where((lane == 0) & (row_iota((length, PAIR)) >= valid), masked_score, 0.0)
    keys[:, :PAIR] = k_ref[...]
    keys[:, PAIR:] = bias.astype(BF16)
    lane = lane_iota((TILE, PAIR))
    upper = lane_iota((TILE, TILE)) > row_iota((TILE, TILE))
    ones = jnp.where(lane == 0, 1.0, 0.0).astype(BF16)

    @pl.when(pair == 0)
    def _():
        lse_ref[...] = jnp.zeros_like(lse_ref)

    for block in range(length // TILE):
        rows = pl.ds(block * TILE, TILE)
        outs = []
        marks = lse_ref[rows, :]
        for head in range(2):
            mine = (lane >= head * HEAD_DIM) & (lane < (head + 1) * HEAD_DIM)
            query = jnp.where(mine, q_ref[rows, :].astype(F32) * HEAD_DIM**-0.5, 0.0).astype(BF16)
            query = jnp.concatenate([query, ones], axis=1)
            near = dot_nt(query, keys[rows, :])
            near = jnp.where(upper, masked_score, near)
            top = jnp.max(near, axis=-1, keepdims=True)
            if block:
                far = dot_nt(query, keys[: block * TILE, :])
                top = jnp.maximum(top, jnp.max(far, axis=-1, keepdims=True))
            near = jnp.exp(near - top)
            total = jnp.sum(near, axis=-1, keepdims=True)
            out = dot(near.astype(BF16), v_ref[rows, :])
            if block:
                far = jnp.exp(far - top)
                total += jnp.sum(far, axis=-1, keepdims=True)
                out += dot(far.astype(BF16), v_ref[: block * TILE, :])
            outs.append(out / total)
            marks = jnp.where(lane == 2 * pair + head, top + jnp.log(total), marks)
        mixed_ref[rows, :] = jnp.where(lane < HEAD_DIM, outs[0], outs[1]).astype(BF16)
        lse_ref[rows, :] = marks


def attend(joint, lengths):
    tokens = joint.shape[0]
    width = joint.shape[1] // 3
    pairs = width // PAIR
    return pl.pallas_call(
        attend_kernel,
        grid_spec=pltpu.PrefetchScalarGridSpec(
            num_scalar_prefetch=1,
            grid=(pairs,),
            in_specs=[
                pl.BlockSpec((tokens, PAIR), lambda p, _: (0, p)),
                pl.BlockSpec((tokens, PAIR), lambda p, _: (0, pairs + p)),
                pl.BlockSpec((tokens, PAIR), lambda p, _: (0, 2 * pairs + p)),
            ],
            out_specs=(
                pl.BlockSpec((tokens, PAIR), lambda p, _: (0, p)),
                pl.BlockSpec((tokens, 128), lambda p, _: (0, 0)),
            ),
            scratch_shapes=[pltpu.VMEM((tokens, 2 * PAIR), BF16)],
        ),
        out_shape=(
            jax.ShapeDtypeStruct((tokens, width), BF16),
            jax.ShapeDtypeStruct((tokens, 128), F32),
        ),
        compiler_params=params("arbitrary"),
    )(lengths, joint, joint, joint)


def middle_kernel(x_ref, mixed_ref, w_ref, n_ref, place_ref, residual_ref, slots_ref, normed, rows):
    rows[...] = norm_rows(n_ref)
    tokens = x_ref.shape[0]
    for start in range(0, tokens, TILE):
        part = pl.ds(start, TILE)
        residual = x_ref[part, :].astype(F32) + dot(mixed_ref[part, :], w_ref[...])
        residual_ref[part, :] = residual
        normal, _ = norm_parts(residual)
        normed[part, :] = (normal * rows[2:3] + rows[3:4]).astype(BF16)
    for start in range(0, slots_ref.shape[0], TILE):
        part = pl.ds(start, TILE)
        slots_ref[part, :] = dot(place_ref[part, :], normed[...]).astype(BF16)


def middle(inputs, mixed, whole, place):
    tokens, width = inputs.shape
    full = lambda shape: pl.BlockSpec(shape, lambda i: (0, 0))
    return pl.pallas_call(
        middle_kernel,
        grid=(1,),
        out_shape=(
            jax.ShapeDtypeStruct((tokens, width), F32),
            jax.ShapeDtypeStruct((place.shape[0], width), BF16),
        ),
        in_specs=[
            full((tokens, width)),
            full((tokens, width)),
            pl.BlockSpec((width, width), lambda i: (0, 3)),
            pl.BlockSpec((width, 128), lambda i: (0, 4 * width // 128)),
            full(place.shape),
        ],
        out_specs=(full((tokens, width)), full((place.shape[0], width))),
        scratch_shapes=[pltpu.VMEM((tokens, width), BF16), pltpu.VMEM((128, width), F32)],
        compiler_params=params("arbitrary"),
    )(inputs, mixed, whole, whole, place)


def expert_kernel(owner, x_ref, g_ref, w_ref, out_ref, back_ref, grads_ref, in_acc, out_acc):
    step = pl.program_id(0)
    groups, _, experts, rows, width = w_ref.shape
    hidden = groups * rows
    tiles = x_ref.shape[0] // TILE

    @pl.when(step == 0)
    def _():
        out_ref[...] = jnp.zeros_like(out_ref)
        back_ref[...] = jnp.zeros_like(back_ref)

    in_acc[...] = jnp.zeros_like(in_acc)
    out_acc[...] = jnp.zeros_like(out_acc)

    def tile_step(tile, carry):
        expert = owner[tile]
        part = pl.ds(pl.multiple_of(tile * TILE, TILE), TILE)
        w_in = w_ref[:, 0, expert].reshape(hidden, width)
        w_out = w_ref[:, 1, expert].reshape(hidden, width)
        tokens = x_ref[part, :]
        cotangent = g_ref[part, :]
        pre = dot_nt(w_in, tokens)
        dact = dot_nt(w_out, cotangent)
        square = pre * pre
        bend = jnp.tanh(gelu_coeff * pre * (1.0 + 0.044715 * square))
        lift = 0.5 * (1.0 + bend)
        act = (pre * lift).astype(BF16)
        slope = lift + 0.5 * pre * (1.0 - bend * bend) * gelu_coeff * (1.0 + 0.134145 * square)
        dpre = (slope * dact).astype(BF16)
        in_acc[expert] += dot(dpre, tokens)
        out_acc[expert] += dot(act, cotangent)
        out_ref[part, :] += dot_tn(act, w_out)
        back_ref[part, :] += dot_tn(dpre, w_in)
        return carry

    lax.fori_loop(0, tiles, tile_step, 0)
    for expert in range(experts):
        grads_ref[:, 0, expert] = in_acc[expert].astype(BF16).reshape(groups, rows, width)
        grads_ref[:, 1, expert] = out_acc[expert].astype(BF16).reshape(groups, rows, width)


def run_experts(owner, slot_inputs, slot_grads, weights):
    count, _, experts, rows, width = weights.shape
    slots = slot_inputs.shape[0]
    groups = max(1, 384 // rows)
    block = (groups,) + weights.shape[1:]
    full = pl.BlockSpec((slots, width), lambda i, _: (0, 0))
    piece = pl.BlockSpec(block, lambda i, _: (i, 0, 0, 0, 0))
    return pl.pallas_call(
        expert_kernel,
        grid_spec=pltpu.PrefetchScalarGridSpec(
            num_scalar_prefetch=1,
            grid=(count // groups,),
            in_specs=[full, full, piece],
            out_specs=(full, full, piece),
            scratch_shapes=[pltpu.VMEM((experts, groups * rows, width), F32)] * 2,
        ),
        out_shape=(
            jax.ShapeDtypeStruct((slots, width), F32),
            jax.ShapeDtypeStruct((slots, width), F32),
            jax.ShapeDtypeStruct(weights.shape, BF16),
        ),
        compiler_params=params("arbitrary"),
    )(owner, slot_inputs, slot_grads, weights)


def split(values):
    high = values.astype(BF16)
    return high, (values - high.astype(F32)).astype(BF16)


def turn_kernel(
    out_ref, back_ref, place_ref, residual_ref, mixed_ref, grad_ref, w_ref, n_ref,
    hidden_ref, dres_ref, dproj_ref, dmixed_ref, delta_ref, wgrad_ref, ngrad_ref, rows,
):
    step = pl.program_id(0)
    width = residual_ref.shape[1]

    @pl.when(step == 0)
    def _():
        rows[...] = norm_rows(n_ref)
        wgrad_ref[...] = jnp.zeros_like(wgrad_ref)
        ngrad_ref[...] = jnp.zeros_like(ngrad_ref)

    place = place_ref[...]
    branch = dot_tn(place, out_ref[...].astype(BF16))
    dnormed = dot_tn(place, back_ref[...].astype(BF16))
    residual = residual_ref[...]
    hidden_ref[...] = (residual + branch).astype(BF16)
    normal, inverse = norm_parts(residual)
    ngrad_ref[0:1] += jnp.sum(dnormed * normal, axis=0, keepdims=True)
    ngrad_ref[1:2] += jnp.sum(dnormed, axis=0, keepdims=True)
    dres = grad_ref[...].astype(F32) + norm_back(dnormed, normal, inverse, rows[2:3])
    dres_ref[...] = dres
    dproj = dres.astype(BF16)
    mixed = mixed_ref[...]
    wgrad_ref[...] += dot_tn(mixed, dproj)
    dmixed = dot_nt(dproj, w_ref[...]).astype(BF16)
    dmixed_ref[...] = dmixed
    heads = (row_iota((width, 128)) // HEAD_DIM == lane_iota((width, 128))).astype(BF16)
    high, low = split(dmixed.astype(F32) * mixed.astype(F32))
    delta_ref[...] = dot(high, heads) + dot(low, heads)


def turn(out, back, place, residual, mixed, grad, whole):
    tokens, width = residual.shape
    slots = out.shape[0]
    row = pl.BlockSpec((TILE, width), lambda i: (i, 0))
    full = lambda shape, *at: pl.BlockSpec(shape, lambda i: at or (0, 0))
    return pl.pallas_call(
        turn_kernel,
        grid=(tokens // TILE,),
        out_shape=(
            jax.ShapeDtypeStruct((tokens, width), BF16),
            jax.ShapeDtypeStruct((tokens, width), F32),
            jax.ShapeDtypeStruct((tokens, width), BF16),
            jax.ShapeDtypeStruct((tokens, width), BF16),
            jax.ShapeDtypeStruct((tokens, 128), F32),
            jax.ShapeDtypeStruct((width, width), F32),
            jax.ShapeDtypeStruct((8, width), F32),
        ),
        in_specs=[
            full((slots, width)),
            full((slots, width)),
            pl.BlockSpec((slots, TILE), lambda i: (0, i)),
            row,
            row,
            row,
            full((width, width), 0, 3),
            full((width, 128), 0, 4 * width // 128),
        ],
        out_specs=(
            row, row, row, row,
            pl.BlockSpec((TILE, 128), lambda i: (i, 0)),
            full((width, width)),
            full((8, width)),
        ),
        scratch_shapes=[pltpu.VMEM((128, width), F32)],
        compiler_params=params("arbitrary"),
    )(out, back, place, residual, mixed, grad, whole, whole)


def column(values, at):
    return jnp.sum(jnp.where(lane_iota(values.shape) == at, values, 0.0), axis=1, keepdims=True)


def extra_lanes(values, more=None):
    high = values.astype(BF16).astype(F32)
    mid = (values - high).astype(BF16).astype(F32)
    low = values - high - mid
    lane = lane_iota((values.shape[0], PAIR))
    out = jnp.where(lane == 0, high, jnp.where(lane == 1, mid, jnp.where(lane == 2, low, 0.0)))
    if more is not None:
        out = jnp.where(lane == 3, more, out)
    return out.astype(BF16)


def attend_back_kernel(
    len_ref, q_ref, k_ref, v_ref, d_ref, lse_ref, delta_ref, dq_ref, dk_ref, dv_ref,
    keys, values, queries, grads, dq_acc,
):
    pair = pl.program_id(0)
    length = q_ref.shape[0]
    valid = len_ref[0]
    lane = lane_iota((length, PAIR))
    late = row_iota((length, PAIR)) >= valid
    marks = jnp.where(lane < 3, 1.0, jnp.where((lane == 3) & late, masked_score, 0.0))
    keys[:, :PAIR] = k_ref[...]
    keys[:, PAIR:] = marks.astype(BF16)
    values[:, :PAIR] = v_ref[...]
    values[:, PAIR:] = jnp.where(lane < 3, 1.0, 0.0).astype(BF16)
    key_rows = jnp.transpose(k_ref[...])
    scaled = (q_ref[...].astype(F32) * HEAD_DIM**-0.5).astype(BF16)
    lower = row_iota((TILE, TILE)) > lane_iota((TILE, TILE))
    half = lane_iota((TILE, PAIR)) < HEAD_DIM
    dq_acc[...] = jnp.zeros_like(dq_acc)
    for head in range(2):
        mine = (lane >= head * HEAD_DIM) & (lane < (head + 1) * HEAD_DIM)
        queries[head, :, :PAIR] = jnp.where(mine, scaled.astype(F32), 0.0).astype(BF16)
        queries[head, :, PAIR:] = extra_lanes(-column(lse_ref[...], 2 * pair + head), 1.0)
        grads[head, :, :PAIR] = jnp.where(mine, d_ref[...].astype(F32), 0.0).astype(BF16)
        grads[head, :, PAIR:] = extra_lanes(-column(delta_ref[...], 2 * pair + head))
    for block in range(length // TILE):
        rows = pl.ds(block * TILE, TILE)
        dks, dvs = [], []
        for head in range(2):
            dk = dv = None
            for start in range(block * TILE, length, TILE):
                later = pl.ds(start, TILE)
                scores = dot_nt(keys[rows, :], queries[head, later, :])
                if start == block * TILE:
                    scores = jnp.where(lower, masked_score, scores)
                probs = jnp.exp(scores)
                dscores = probs * dot_nt(values[rows, :], grads[head, later, :])
                probs, dscores = probs.astype(BF16), dscores.astype(BF16)
                more_v = dot(probs, grads[head, later, :PAIR])
                more_k = dot(dscores, queries[head, later, :PAIR])
                dv = more_v if dv is None else dv + more_v
                dk = more_k if dk is None else dk + more_k
                spot = pl.ds(head * HEAD_DIM, HEAD_DIM)
                dq_acc[spot, start : start + TILE] += dot(
                    key_rows[head * HEAD_DIM : (head + 1) * HEAD_DIM, block * TILE : (block + 1) * TILE],
                    dscores,
                )
            dks.append(dk)
            dvs.append(dv)
        dk_ref[rows, :] = jnp.where(half, dks[0], dks[1]).astype(BF16)
        dv_ref[rows, :] = jnp.where(half, dvs[0], dvs[1]).astype(BF16)
    dq_ref[...] = jnp.transpose(dq_acc[...] * HEAD_DIM**-0.5).astype(BF16)


def attend_back(joint, dmixed, lse, delta, lengths):
    tokens, width = dmixed.shape
    pairs = width // PAIR
    narrow = pl.BlockSpec((tokens, PAIR), lambda p, _: (0, p))
    full = pl.BlockSpec((tokens, 128), lambda p, _: (0, 0))
    return pl.pallas_call(
        attend_back_kernel,
        grid_spec=pltpu.PrefetchScalarGridSpec(
            num_scalar_prefetch=1,
            grid=(pairs,),
            in_specs=[
                narrow,
                pl.BlockSpec((tokens, PAIR), lambda p, _: (0, pairs + p)),
                pl.BlockSpec((tokens, PAIR), lambda p, _: (0, 2 * pairs + p)),
                narrow,
                full,
                full,
            ],
            out_specs=(narrow,) * 3,
            scratch_shapes=[
                pltpu.VMEM((tokens, 2 * PAIR), BF16),
                pltpu.VMEM((tokens, 2 * PAIR), BF16),
                pltpu.VMEM((2, tokens, 2 * PAIR), BF16),
                pltpu.VMEM((2, tokens, 2 * PAIR), BF16),
                pltpu.VMEM((PAIR, tokens), F32),
            ],
        ),
        out_shape=(jax.ShapeDtypeStruct((tokens, width), BF16),) * 3,
        compiler_params=params("arbitrary"),
    )(lengths, joint, joint, joint, dmixed, lse, delta)


def finish_kernel(
    dq_ref, dk_ref, dv_ref, normed_ref, w_ref, n_ref, x_ref, dres_ref, wgrad_ref, ngrad_ref,
    input_ref, pack_ref, rows, acc, sums,
):
    step = pl.program_id(0)
    width = x_ref.shape[1]

    @pl.when(step == 0)
    def _():
        rows[...] = norm_rows(n_ref)
        acc[...] = jnp.zeros_like(acc)
        sums[...] = jnp.zeros_like(sums)
        sums[2:4, :] = ngrad_ref[0:2, :]

    normed = normed_ref[...]
    dnormed = None
    for number, ref in enumerate((dq_ref, dk_ref, dv_ref)):
        part = slice(number * width, (number + 1) * width)
        value = ref[...]
        more = dot_nt(value, w_ref[:, part])
        dnormed = more if dnormed is None else dnormed + more
        acc[:, part] += dot_tn(normed, value)
    normal, inverse = norm_parts(x_ref[...].astype(F32))
    sums[0:1] += jnp.sum(dnormed * normal, axis=0, keepdims=True)
    sums[1:2] += jnp.sum(dnormed, axis=0, keepdims=True)
    input_ref[...] = (dres_ref[...] + norm_back(dnormed, normal, inverse, rows[0:1])).astype(BF16)

    @pl.when(step == pl.num_programs(0) - 1)
    def _():
        pack_ref[:, : 3 * width] = acc[...].astype(BF16)
        pack_ref[:, 3 * width : 4 * width] = wgrad_ref[...].astype(BF16)
        pack_ref[:, 4 * width :] = jnp.transpose(sums[...]).astype(BF16)


def finish(dqkv, normed, whole, inputs, dres, wgrad, ngrad):
    tokens, width = inputs.shape
    row = pl.BlockSpec((TILE, width), lambda i: (i, 0))
    full = lambda shape, *at: pl.BlockSpec(shape, lambda i: at or (0, 0))
    return pl.pallas_call(
        finish_kernel,
        grid=(tokens // TILE,),
        out_shape=(
            jax.ShapeDtypeStruct((tokens, width), BF16),
            jax.ShapeDtypeStruct((width, 4 * width + 128), BF16),
        ),
        in_specs=[
            row, row, row, row,
            full((width, 3 * width)),
            full((width, 128), 0, 4 * width // 128),
            row, row,
            full((width, width)),
            full((8, width)),
        ],
        out_specs=(row, full((width, 4 * width + 128))),
        scratch_shapes=[
            pltpu.VMEM((128, width), F32),
            pltpu.VMEM((width, 3 * width), F32),
            pltpu.VMEM((128, width), F32),
        ],
        compiler_params=params("arbitrary"),
    )(*dqkv, normed, whole, whole, inputs, dres, wgrad, ngrad)


def route(chosen, tokens):
    slots = tokens + TILE
    second = chosen.astype(jnp.int32)
    ones = jnp.cumsum(second)
    zeros = jnp.cumsum(1 - second)
    edge = (zeros[-1] + TILE - 1) // TILE * TILE
    spot = jnp.where(second == 0, zeros - 1, edge + ones - 1)
    place = (jnp.arange(slots, dtype=jnp.int32)[:, None] == spot[None, :]).astype(BF16)
    owner = (jnp.arange(slots // TILE, dtype=jnp.int32) * TILE >= edge).astype(jnp.int32)
    return place, owner


def body(
    cube,
    hidden_in,
    lengths,
    expert_ids,
    norm1_gain,
    norm1_bias,
    qkv_weight,
    attn_out_weight,
    norm2_gain,
    norm2_bias,
    expert_in,
    expert_out,
    out_grad,
):
    tokens, width = hidden_in.shape
    rows = qkv_weight.shape[0]
    count = cube.count
    norms = jnp.stack([norm1_gain, norm1_bias, norm2_gain, norm2_bias], 1)
    small = jnp.concatenate(
        [qkv_weight, attn_out_weight, jnp.pad(norms, ((0, 0), (0, 124)))], axis=1
    )
    large = jnp.stack([expert_in, expert_out], 0).transpose(0, 2, 1, 3)
    small_all, large_all = gather_all(cube, small, large)
    whole = small_all.reshape(count * rows, small.shape[1])
    place, owner = route(expert_ids[:, 0], tokens)
    slot_grads = jnp.dot(place, out_grad, preferred_element_type=F32).astype(BF16)
    normed, joint = project(hidden_in, whole)
    mixed, lse = attend(joint, lengths)
    residual, slot_inputs = middle(hidden_in, mixed, whole, place)
    out, back, grads = run_experts(owner, slot_inputs, slot_grads, large_all)
    shape = (count, 4, grads.shape[3], width)
    expert_total = reduce_all(
        cube,
        grads.reshape(shape),
        ((0, width // 2, 0), (width // 2, width, 1)),
        1,
    ).reshape(grads.shape[1:])
    hidden_out, dres, dproj, dmixed, delta, wgrad, ngrad = turn(
        out, back, place, residual, mixed, out_grad, whole
    )
    dqkv = attend_back(joint, dmixed, lse, delta, lengths)
    input_grad, pack = finish(dqkv, normed, whole, hidden_in, dres, wgrad, ngrad)
    columns = pack.shape[1]
    lanes = columns // 128
    first, second = 128 * (lanes * 2 // 5), 128 * (lanes * 4 // 5)
    total = reduce_all(
        cube,
        pack.reshape(count, 1, rows, columns),
        ((0, first, 0), (first, second, 1), (second, columns, 2)),
        2,
    )[0]
    return (
        hidden_out,
        input_grad,
        total[:, 4 * width],
        total[:, 4 * width + 1],
        total[:, : 3 * width],
        total[:, 3 * width : 4 * width],
        total[:, 4 * width + 2],
        total[:, 4 * width + 3],
        expert_total[0].transpose(1, 0, 2),
        expert_total[1].transpose(1, 0, 2),
    )


def solution(mesh):
    cube = Cube(mesh.shape["dp"], mesh.shape["fsdp"])
    both = ("dp", "fsdp")
    vector, matrix, cube3 = P(both), P(both, None), P(both, None, None)
    in_specs = (
        matrix, vector, matrix, vector, vector, matrix, matrix, vector, vector, cube3, cube3, matrix,
    )
    out_specs = (
        matrix, matrix, vector, vector, matrix, matrix, vector, vector, cube3, cube3,
    )
    return jax.shard_map(
        functools.partial(body, cube),
        mesh=mesh,
        in_specs=in_specs,
        out_specs=out_specs,
        check_vma=False,
    )
```
